512 devices in a mesh: sec: 64 (over x, y, core), mp: 8 (over z).
Axes of the slice: x: 4, y: 8, z: 8, core: 2. Of those that a mesh axis runs over, the one named last changes fastest.
Arguments:
- inputs: bfloat16 [8192, 2048], P('sec'), may hold values from -6 to 6
- expert_w: bfloat16 [8, 2048, 1024], P('mp', 'sec'), may hold values from -0.125 to 0.125
- gate_w: bfloat16 [2048, 6, 8], replicated, may hold values from -0.125 to 0.125
- tower_up: bfloat16 [64, 1024, 4096], P('sec', None, 'mp'), as said below
- tower_out: bfloat16 [64, 4096], P('sec', 'mp'), as said below
- sections: int32 [64], replicated, may hold values from 0 to 5, as said below
- tasks: int32 [8192, 6], P('sec'), may hold values from 0 to 1, as said below
- labels: int32 [8192, 6], P('sec'), may hold values 0 or 1
Outputs:
- input_grad: bfloat16 [8192, 2048], P('sec', 'mp')
The draws below stay inside these ranges and needn't reach their ends.
Inputs may be any that keep to these rules, and one draw needn't show every extreme that they name: `sections`: each task owns one run of consecutive indices, the runs in task order, every task at least one index. `tasks`: in each aligned block of 128 examples, task t has at most 4 times as many examples as its section has indices of sec; every task reaches this bound in some block. `tower_up`: all indices of one section hold equal copies. `tower_out`: all indices of one section hold equal copies.
All inputs are finite; a program needn't handle non-finite values. No bound on the sum of `labels` on one device may be relied on, other than what follows from the above.
Results may differ from the reference program's by a relative error of at most 0.024.
Values may be sent and summed in bfloat16 or wider, within the bound.
No kernel may reach another device: no remote copies, remote signals or barrier semaphores. Data moves between devices by JAX's collectives and lax.ppermute only.
A program may use at most 64 MiB of HBM per device.

```python
import jax
import jax.numpy as jnp
from jax import lax

DIN = 2048
EW = 1024
TH = 4096
TASKS = 6
EX_DEV = 128
EXPERTS = 8
EXAMPLES = 8192
SECS = 64


def section_layout(key):
    shares = jnp.array([4, 3, 2, 2, 1, 1], jnp.int32)
    order = jax.random.permutation(jax.random.fold_in(key, 7), TASKS)
    base = SECS * shares // 13
    base = base.at[0].add(SECS - jnp.sum(base))
    counts = jnp.zeros((TASKS,), jnp.int32).at[order].set(base)
    ends = jnp.cumsum(counts)
    index = jnp.arange(SECS, dtype=jnp.int32)
    return jnp.sum((index[:, None] >= ends[None, :]).astype(jnp.int32), axis=1)


def draw_sections(key, part):
    return section_layout(key)


def draw_tasks(key, part):
    layout = section_layout(key)
    counts = jnp.sum((layout[None, :] == jnp.arange(TASKS, dtype=jnp.int32)[:, None]).astype(jnp.int32), axis=1)
    top = counts * (2 * EX_DEV // SECS)
    low = top // 2
    raw = jax.random.randint(jax.random.fold_in(key, 11), (SECS, TASKS), 0, 1 << 20)
    amount = raw % (top - low + 1)[None, :] + low[None, :]
    star = jax.random.randint(jax.random.fold_in(key, 13), (TASKS,), 0, SECS)
    amount = jnp.where(jnp.arange(SECS, dtype=jnp.int32)[:, None] == star[None, :], top[None, :], amount)
    keys = jax.random.split(jax.random.fold_in(key, 17), SECS * TASKS)
    orders = jax.vmap(lambda one: jax.random.permutation(one, EX_DEV))(keys).reshape(SECS, TASKS, EX_DEV)
    member = (orders < amount[:, :, None]).astype(jnp.int32)
    return jnp.transpose(member, (0, 2, 1)).reshape(SECS * EX_DEV, TASKS)


def draw_tower_up(key, part):
    layout = section_layout(key)
    base = jax.random.normal(jax.random.fold_in(key, 23), (TASKS, EW, TH), jnp.float32) * EW ** (-0.5)
    return base[layout].astype(jnp.bfloat16)


def draw_tower_out(key, part):
    layout = section_layout(key)
    base = jax.random.normal(jax.random.fold_in(key, 29), (TASKS, TH), jnp.float32) * (8.0 * TH ** (-0.5))
    return base[layout].astype(jnp.bfloat16)


def set_ends(values, rng, low, largest):
    spot = [jax.random.randint(jax.random.fold_in(rng, axis), (), 0, length) for axis, length in enumerate(values.shape)]
    widest = values.shape.index(max(values.shape))
    beside = spot[:widest] + [(spot[widest] + 1) % values.shape[widest]] + spot[widest + 1:]
    return values.at[tuple(spot)].set(low).at[tuple(beside)].set(largest)


def block_levels(rng, extent, shards, smallest, high):
    def one(axis_at, shards_of):
        draws = jax.random.uniform(jax.random.fold_in(jax.random.fold_in(rng, 6), axis_at), (shards_of,), jnp.float32, smallest / len(shards), high / len(shards))
        return jnp.repeat(jnp.exp(draws), extent[axis_at] // shards_of).reshape((-1,) + (1,) * (len(extent) - axis_at - 1))

    gain = one(*shards[0])
    for cut in shards[1:]:
        gain = gain * one(*cut)
    return gain


def noise(rng, dims, spread, reach, cuts=(), kind=jnp.bfloat16):
    factor_of = block_levels(rng, dims, cuts, -0.22, 0.18) if cuts else 1.0
    values = jax.random.normal(rng, dims, jnp.float32) * spread * factor_of
    return jnp.minimum(jnp.maximum(values, -reach), reach).astype(kind)


def setup_inputs(seed: int = 0) -> dict:
    streams_of = jax.random.split(jax.random.key(seed), 9)
    return {
        "inputs": noise(streams_of[0], (EXAMPLES, DIN), 1.0, 6.0, ((0, 64),)),
        "expert_w": noise(streams_of[1], (EXPERTS, DIN, EW), DIN ** -0.5, 0.125, ((0, 8), (1, 64))),
        "gate_w": noise(streams_of[2], (DIN, TASKS, EXPERTS), DIN ** -0.5, 0.125),
        "tower_up": draw_tower_up(jax.random.fold_in(streams_of[8], 71), 0),
        "tower_out": draw_tower_out(jax.random.fold_in(streams_of[8], 71), 0),
        "sections": draw_sections(jax.random.fold_in(streams_of[8], 71), 0),
        "tasks": draw_tasks(jax.random.fold_in(streams_of[8], 71), 0),
        "labels": set_ends((jax.random.randint(streams_of[7], (EXAMPLES, TASKS), 0, 2) < 1).astype(jnp.int32), jax.random.fold_in(streams_of[7], 1), 0, 1),
    }


loss_scale = 64.0


def silu_slope(value, sig):
    return sig * (1.0 + value * (1.0 - sig))


def reference(inputs, expert_w, gate_w, tower_up, tower_out, sections, tasks, labels):
    highest = lax.Precision.HIGHEST
    gate_logit = jnp.einsum("nd,dtk->ntk", inputs.astype(jnp.float32), gate_w.astype(jnp.float32), precision=highest)
    raised = jnp.exp(gate_logit)
    gates = raised / jnp.sum(raised, axis=2, keepdims=True)
    pre = jnp.stack([jnp.dot(inputs, expert_w[k], preferred_element_type=jnp.float32) for k in range(EXPERTS)])
    sig_pre = jax.nn.sigmoid(pre)
    expert_out = (pre * sig_pre).astype(jnp.bfloat16)
    mixture = jnp.einsum("ntk,kne->nte", gates, expert_out.astype(jnp.float32), precision=highest).astype(jnp.bfloat16)
    task_ids = jnp.arange(TASKS).astype(jnp.int32)
    member = jnp.sum((sections[None, :] < task_ids[:, None]).astype(jnp.int32), axis=1)
    alive = tasks.astype(jnp.float32)
    target = labels.astype(jnp.float32)
    grads = []
    for task in range(TASKS):
        up_w = tower_up[member[task]]
        out_w = tower_out[member[task]].astype(jnp.float32)
        act = jnp.dot(mixture[:, task], up_w, preferred_element_type=jnp.float32)
        sig_act = jax.nn.sigmoid(act)
        logit = jnp.sum(act * sig_act * out_w[None, :], axis=1)
        slope = loss_scale * (jax.nn.sigmoid(logit) - target[:, task]) * alive[:, task]
        act_grad = (slope[:, None] * out_w[None, :] * silu_slope(act, sig_act)).astype(jnp.bfloat16)
        grads.append(jnp.dot(act_grad, up_w.T, preferred_element_type=jnp.float32).astype(jnp.bfloat16))
    mixture_grad = jnp.stack(grads, axis=1)
    expert_grad = jnp.einsum("ntk,nte->kne", gates, mixture_grad.astype(jnp.float32), precision=highest)
    gate_grad = jnp.einsum("nte,kne->ntk", mixture_grad.astype(jnp.float32), expert_out.astype(jnp.float32), precision=highest)
    gate_logit_grad = gates * (gate_grad - jnp.sum(gates * gate_grad, axis=2, keepdims=True))
    pre_grad = (expert_grad * silu_slope(pre, sig_pre)).astype(jnp.bfloat16)
    total = jnp.einsum("ntk,dtk->nd", gate_logit_grad, gate_w.astype(jnp.float32), precision=highest)
    for k in range(EXPERTS):
        total = total + jnp.dot(pre_grad[k], expert_w[k].T, preferred_element_type=jnp.float32)
    return total.astype(jnp.bfloat16)
```

```python
import jax
import jax.numpy as jnp
from jax import lax
from jax.sharding import Mesh, PartitionSpec as P

loss_scale = 64.0
NX, NY, NC = 4, 8, 2


def silu_slope(value, sig):
    return sig * (1.0 + value * (1.0 - sig))


def split_two(value):
    high = lax.reduce_precision(value, 8, 7)
    return high.astype(jnp.bfloat16), (value - high).astype(jnp.bfloat16)


def per_device(inputs, expert_w, gate_w, tower_up, tower_out, sections, tasks, labels):
    f32, bf16 = jnp.float32, jnp.bfloat16
    rows, din = inputs.shape
    tn = tasks.shape[1]
    n_mp = lax.axis_size("mp")
    n_sec = NX * NY * NC
    kn = gate_w.shape[2]
    part_d, width = expert_w.shape[1:]
    cols = width // n_mp
    pair_slots = 2 * rows // n_sec
    slots = n_sec * pair_slots
    sec_axes = ("x", "y", "c")

    block = expert_w[0].reshape(part_d, n_mp, cols).transpose(1, 0, 2)
    block = jnp.broadcast_to(block[None], (NY, n_mp, part_d, cols))
    part = lax.all_to_all(
        block.reshape(NY * n_mp, part_d, cols), ("y", "mp"), 0, 0, tiled=True
    )
    wide = lax.all_to_all(
        jnp.broadcast_to(part[None], (NX,) + part.shape), "x", 0, 0, tiled=True
    )
    other = lax.ppermute(wide, "c", [(0, 1), (1, 0)])
    core = lax.axis_index("c")
    zero = jnp.where(core == 0, wide, other).reshape(NX * NY, 1, kn, part_d, cols)
    one = jnp.where(core == 0, other, wide).reshape(NX * NY, 1, kn, part_d, cols)
    whole = jnp.concatenate([zero, one], axis=1).reshape(n_sec, kn, part_d, cols)
    w_all = whole.transpose(0, 2, 1, 3).reshape(din, kn * cols)

    gate_logit = jnp.einsum("nd,dtk->ntk", inputs, gate_w, preferred_element_type=f32)
    raised = jnp.exp(gate_logit)
    gates = raised / jnp.sum(raised, axis=2, keepdims=True)
    task_ids = jnp.arange(tn, dtype=jnp.int32)
    members = jnp.sum((sections[None, :] == task_ids[:, None]).astype(jnp.int32), axis=1)
    first = jnp.sum((sections[None, :] < task_ids[:, None]).astype(jnp.int32), axis=1)
    ranks = jnp.cumsum(tasks, axis=0) - tasks
    turn = jnp.zeros_like(ranks)
    for step in range(1, pair_slots):
        turn = turn + (ranks >= step * members[None, :]).astype(jnp.int32)
    place = (first[None, :] + ranks - turn * members[None, :]) * pair_slots + turn
    place = jnp.where(tasks > 0, place, slots).reshape(1, rows * tn)
    pick = (place == jnp.arange(slots, dtype=jnp.int32)[:, None]).astype(bf16)

    pre = jnp.dot(inputs, w_all, preferred_element_type=f32).reshape(rows, kn, cols)
    sig_pre = jax.nn.sigmoid(pre)
    expert_out = (pre * sig_pre).astype(bf16)
    wide_out = expert_out.astype(f32)
    mixture = gates[:, :, 0, None] * wide_out[:, None, 0]
    for k in range(1, kn):
        mixture = mixture + gates[:, :, k, None] * wide_out[:, None, k]
    mixture = mixture.astype(bf16).reshape(rows * tn, cols)
    sent = jnp.dot(pick, mixture, preferred_element_type=f32).astype(bf16)
    sent = jnp.broadcast_to(
        sent.reshape(1, n_sec, pair_slots, cols), (n_mp, n_sec, pair_slots, cols)
    ).reshape(n_mp * n_sec, pair_slots, cols)
    arrived = lax.all_to_all(sent, ("mp",) + sec_axes, 0, 0, tiled=True)

    up = tower_up[0]
    out_w = tower_out[0].astype(f32)
    rows_in = arrived.reshape(n_mp, slots, cols).transpose(1, 0, 2).reshape(slots, width)
    act = jnp.dot(rows_in, up, preferred_element_type=f32)
    sig_act = jax.nn.sigmoid(act)
    logit_part = jnp.sum(act * sig_act * out_w[None, :], axis=1)
    act_grad = (out_w[None, :] * silu_slope(act, sig_act)).astype(bf16)
    back = lax.dot_general(
        act_grad, up, (((1,), (1,)), ((), ())), preferred_element_type=f32
    ).astype(bf16)
    back = back.reshape(slots, n_mp, cols).transpose(1, 0, 2)
    high, low = split_two(logit_part)
    extra = jnp.concatenate([high.reshape(-1, cols), low.reshape(-1, cols)], axis=0)
    n_extra = extra.shape[0]
    extra = jnp.concatenate([extra, jnp.zeros((16 - n_extra, cols), bf16)], axis=0)
    extra = jnp.broadcast_to(extra[None], (n_mp, 16, cols))
    summed = lax.all_to_all(jnp.concatenate([back, extra], axis=1), "mp", 0, 0, tiled=True)
    total = jnp.sum(summed.astype(f32), axis=0)
    logit = (total[slots : slots + n_extra // 2] + total[slots + n_extra // 2 : slots + n_extra])
    high, low = split_two(logit.reshape(n_sec, pair_slots))
    tail = jnp.concatenate([high, low], axis=1)
    tail = jnp.pad(tail, ((0, 0), (0, cols - 2 * pair_slots)))[:, None]
    body = total[:slots].astype(bf16).reshape(n_sec, pair_slots, cols)
    fill = jnp.zeros((n_sec, 8 - pair_slots - 1, cols), bf16)
    home = lax.all_to_all(
        jnp.concatenate([body, tail, fill], axis=1), sec_axes, 0, 0, tiled=True
    )
    grads = home[:, :pair_slots].reshape(slots, cols)
    logits = home[:, pair_slots, : 2 * pair_slots].reshape(n_sec, 2, pair_slots)
    logits = logits.transpose(0, 2, 1).reshape(slots, 2)

    stacked = jnp.concatenate([grads, logits, jnp.zeros((slots, cols - 2), bf16)], axis=1)
    rows_back = lax.dot_general(
        pick, stacked, (((0,), (0,)), ((), ())), preferred_element_type=f32
    ).reshape(rows, tn, 2 * cols)
    logit_home = rows_back[:, :, cols] + rows_back[:, :, cols + 1]
    slope = loss_scale * (jax.nn.sigmoid(logit_home) - labels.astype(f32)) * tasks.astype(f32)
    mixture_grad = (slope[:, :, None] * rows_back[:, :, :cols]).astype(bf16).astype(f32)
    expert_grad = gates[:, 0, :, None] * mixture_grad[:, 0, None]
    for task in range(1, tn):
        expert_grad = expert_grad + gates[:, task, :, None] * mixture_grad[:, task, None]
    gate_grad = jnp.sum(mixture_grad[:, :, None, :] * wide_out[:, None, :, :], axis=3)
    spread = jnp.sum(gates * gate_grad, axis=2, keepdims=True)
    gate_logit_grad = gates * (gate_grad - spread)
    pre_grad = (expert_grad * silu_slope(pre, sig_pre)).astype(bf16).reshape(rows, kn * cols)
    gate_part = jnp.dot(
        gate_logit_grad.reshape(rows, tn * kn),
        gate_w.astype(f32).reshape(din, tn * kn).T,
        precision=lax.Precision.HIGHEST,
    )
    input_part = lax.dot_general(
        pre_grad, w_all, (((1,), (1,)), ((), ())), preferred_element_type=f32
    )
    partial = (input_part + gate_part).astype(bf16)
    partial = partial.reshape(rows, n_mp, din // n_mp).transpose(1, 0, 2)
    pieces = lax.all_to_all(partial, "mp", 0, 0, tiled=True)
    return jnp.sum(pieces.astype(f32), axis=0).astype(bf16)


def solution(mesh):
    grid = Mesh(
        mesh.devices.reshape(NX, NY, NC, mesh.shape["mp"]), ("x", "y", "c", "mp")
    )
    sec = ("x", "y", "c")
    in_specs = (
        P(sec, None),
        P("mp", sec, None),
        P(),
        P(sec, None, "mp"),
        P(sec, "mp"),
        P(),
        P(sec, None),
        P(sec, None),
    )
    return jax.shard_map(
        per_device, mesh=grid, in_specs=in_specs, out_specs=P(sec, "mp"), check_vma=False
    )
```

```python
import jax
import jax.numpy as jnp
from jax import lax
from jax.experimental import pallas as pl
from jax.experimental.pallas import tpu as pltpu
from jax.sharding import Mesh, PartitionSpec as P

loss_scale = 64.0
NX, NY, NC = 4, 8, 2


def silu_slope(value, sig):
    return sig * (1.0 + value * (1.0 - sig))


def split_two(value):
    high = lax.reduce_precision(value, 8, 7)
    return high.astype(jnp.bfloat16), (value - high).astype(jnp.bfloat16)


def group_sum(value, group):
    n = value.shape[1]
    row = lax.broadcasted_iota(jnp.int32, (n, n), 0) // group
    col = lax.broadcasted_iota(jnp.int32, (n, n), 1) // group
    ones = (row == col).astype(jnp.float32)
    return jnp.dot(
        value, ones, precision=lax.Precision.HIGHEST, preferred_element_type=jnp.float32
    )


def gate_kernel(tn, kn, pair_slots):
    f32, bf16 = jnp.float32, jnp.bfloat16

    def kernel(x_ref, gw_ref, sec_ref, task_ref, gate_ref, row_ref, col_ref):
        logit = jnp.dot(x_ref[...], gw_ref[...], preferred_element_type=f32)
        raised = jnp.exp(logit)
        gate_ref[...] = raised / group_sum(raised, kn)

        n_sec = sec_ref.shape[1]
        rows = task_ref.shape[0]
        sec_row = sec_ref[...]
        task = task_ref[...].astype(f32)
        task16 = task.astype(bf16)
        one = lax.broadcasted_iota(jnp.int32, (rows, rows), 0)
        two = lax.broadcasted_iota(jnp.int32, (rows, rows), 1)
        below = (two < one).astype(f32).astype(bf16)
        above = (one < two).astype(f32).astype(bf16)
        same = (one == two).astype(f32).astype(bf16)
        across = (((0,), (0,)), ((), ()))
        rank_col = jnp.dot(below, task16, preferred_element_type=f32)
        rank_row = lax.dot_general(task16, above, across, preferred_element_type=f32)
        task_row = lax.dot_general(task16, same, across, preferred_element_type=f32)

        ids_row = lax.broadcasted_iota(jnp.int32, (tn, n_sec), 0)
        hit = (sec_row == ids_row).astype(f32)
        less = (sec_row < ids_row).astype(f32)
        member_col = jnp.sum(hit, axis=1, keepdims=True)
        first_col = jnp.sum(less, axis=1, keepdims=True)
        eye = lax.broadcasted_iota(jnp.int32, (tn, tn), 0) == lax.broadcasted_iota(
            jnp.int32, (tn, tn), 1
        )
        member_row = jnp.sum(jnp.where(eye, member_col, 0.0), axis=0, keepdims=True)
        first_row = jnp.sum(jnp.where(eye, first_col, 0.0), axis=0, keepdims=True)

        def find(rank, member, first, active):
            turn = jnp.zeros_like(rank)
            for step in range(1, pair_slots):
                turn = turn + (rank >= step * member).astype(f32)
            target = first + rank - turn * member
            return jnp.where(active > 0.5, target, -1000.0), turn

        target, turn = find(rank_row, member_col, first_col, task_row)
        row_ref[0:tn, :] = target
        row_ref[tn : 2 * tn, :] = turn
        target, turn = find(rank_col, member_row, first_row, task)
        col_ref[:, 0:tn] = target
        col_ref[:, tn : 2 * tn] = turn

    return kernel


def load_weights(core_ref, own_ref, other_ref, w_ref, sems):
    def run(own_at, finish):
        first = pltpu.make_async_copy(own_ref, w_ref.at[:, own_at], sems.at[0])
        second = pltpu.make_async_copy(other_ref, w_ref.at[:, 1 - own_at], sems.at[1])
        if finish:
            first.wait()
            second.wait()
        else:
            first.start()
            second.start()

    def both(finish):
        @pl.when(core_ref[0] == 0)
        def _():
            run(0, finish)

        @pl.when(core_ref[0] != 0)
        def _():
            run(1, finish)

    return lambda: both(False), lambda: both(True)


def pair_weights(w_ref, k, lo, hi):
    part_d, cols = w_ref.shape[3:]
    count = (hi - lo) * w_ref.shape[1] * part_d
    return jnp.concatenate(
        [w_ref[lo:hi, :, k + i].reshape(count, cols) for i in range(2)], axis=1
    )


def forward_kernel(tn, kn, pair_slots, n_mp):
    f32, bf16 = jnp.float32, jnp.bfloat16

    def kernel(core_ref, own_ref, other_ref, x_ref, gate_ref, row_ref, sent_ref, pre_ref, w_ref, sems):
        start, wait = load_weights(core_ref, own_ref, other_ref, w_ref, sems)
        start()
        rows = x_ref.shape[0]
        slots, cols = sent_ref.shape[1:]
        slot_id = lax.broadcasted_iota(jnp.int32, (slots, rows), 0).astype(f32)
        picks = []
        for t in range(tn):
            place = row_ref[t : t + 1, :] * pair_slots + row_ref[tn + t : tn + t + 1, :]
            picks.append((slot_id == place).astype(f32).astype(bf16))
        pick = jnp.concatenate(picks, axis=1)
        wait()
        x = x_ref[...]
        mix = [jnp.zeros((rows, cols), f32) for _ in range(tn)]
        for k in range(0, kn, 2):
            pre = jnp.dot(
                x, pair_weights(w_ref, k, 0, w_ref.shape[0]), preferred_element_type=f32
            )
            pre_ref[:, k * cols : (k + 2) * cols] = pre
            out = (pre * jax.nn.sigmoid(pre)).astype(bf16).astype(f32)
            for i in range(2):
                part = out[:, i * cols : (i + 1) * cols]
                for t in range(tn):
                    at = t * kn + k + i
                    mix[t] = mix[t] + gate_ref[:, at : at + 1] * part
        stack = jnp.concatenate([m.astype(bf16) for m in mix], axis=0)
        sent = jnp.dot(pick, stack, preferred_element_type=f32).astype(bf16)
        for m in range(n_mp):
            sent_ref[m] = sent

    return kernel


def backward_kernel(tn, kn, pair_slots, n_mp):
    f32, bf16 = jnp.float32, jnp.bfloat16

    def kernel(
        core_ref, own_ref, other_ref, home_ref, gate_ref, col_ref, pre_ref,
        label_ref, task_ref, gw_ref, out_ref, w_ref, sems,
    ):
        start, wait = load_weights(core_ref, own_ref, other_ref, w_ref, sems)
        start()
        total, cols = home_ref.shape
        rows = gate_ref.shape[0]
        home = home_ref[...]
        lane = lax.broadcasted_iota(jnp.int32, (rows, total), 1).astype(f32)
        lane_c = lax.broadcasted_iota(jnp.int32, (rows, cols), 1).astype(f32)
        grads = []
        for t in range(tn):
            target = col_ref[:, t : t + 1] * 8.0
            turn = col_ref[:, tn + t : tn + t + 1]
            pick = (lane == target + turn).astype(f32).astype(bf16)
            pick_tail = (lane == target + pair_slots).astype(f32).astype(bf16)
            got = jnp.dot(pick, home, preferred_element_type=f32)
            tail = jnp.dot(pick_tail, home, preferred_element_type=f32)
            chosen = (lane_c == turn) | (lane_c == turn + pair_slots)
            logit = jnp.sum(jnp.where(chosen, tail, 0.0), axis=1, keepdims=True)
            label = label_ref[:, t : t + 1].astype(f32)
            alive = task_ref[:, t : t + 1].astype(f32)
            slope = loss_scale * (jax.nn.sigmoid(logit) - label) * alive
            grads.append((slope * got).astype(bf16).astype(f32))
        gates = gate_ref[...]
        gate_grad = jnp.zeros((rows, tn * kn), f32)
        lane_g = lax.broadcasted_iota(jnp.int32, (rows, tn * kn), 1)
        pre_grads = []
        for k in range(kn):
            pre = pre_ref[:, k * cols : (k + 1) * cols]
            sig = jax.nn.sigmoid(pre)
            out = (pre * sig).astype(bf16).astype(f32)
            grad = jnp.zeros((rows, cols), f32)
            for t in range(tn):
                at = t * kn + k
                grad = grad + gate_ref[:, at : at + 1] * grads[t]
                dot = jnp.sum(grads[t] * out, axis=1, keepdims=True)
                gate_grad = jnp.where(lane_g == at, dot, gate_grad)
            pre_grads.append((grad * silu_slope(pre, sig)).astype(bf16))
        spread = group_sum(gates * gate_grad, kn)
        logit_grad = gates * (gate_grad - spread)
        high = logit_grad.astype(bf16)
        low = (logit_grad - high.astype(f32)).astype(bf16)
        both = jnp.concatenate([high, low], axis=0)
        pre_grad = [jnp.concatenate(pre_grads[k : k + 2], axis=1) for k in range(0, kn, 2)]
        wait()
        per = w_ref.shape[0] // n_mp
        width = out_ref.shape[2]
        contract = (((1,), (1,)), ((), ()))
        for m in range(n_mp):
            gw = gw_ref[m * width : (m + 1) * width, :]
            gated = lax.dot_general(both, gw, contract, preferred_element_type=f32)
            acc = gated[:rows] + gated[rows:]
            for k in range(0, kn, 2):
                w = pair_weights(w_ref, k, m * per, (m + 1) * per)
                acc = acc + lax.dot_general(
                    pre_grad[k // 2], w, contract, preferred_element_type=f32
                )
            out_ref[m] = acc.astype(bf16)

    return kernel


def per_device(inputs, expert_w, gate_w, tower_up, tower_out, sections, tasks, labels):
    f32, bf16 = jnp.float32, jnp.bfloat16
    rows, din = inputs.shape
    tn = tasks.shape[1]
    n_mp = lax.axis_size("mp")
    n_sec = NX * NY * NC
    kn = gate_w.shape[2]
    part_d, width = expert_w.shape[1:]
    cols = width // n_mp
    pair_slots = 2 * rows // n_sec
    slots = n_sec * pair_slots
    sec_axes = ("x", "y", "c")

    block = expert_w[0].reshape(part_d, n_mp, cols).transpose(1, 0, 2)
    block = jnp.broadcast_to(block[None], (NY, n_mp, part_d, cols))
    part = lax.all_to_all(
        block.reshape(NY * n_mp, part_d, cols), ("y", "mp"), 0, 0, tiled=True
    )
    wide = lax.all_to_all(
        jnp.broadcast_to(part[None], (NX,) + part.shape), "x", 0, 0, tiled=True
    )
    other = lax.ppermute(wide, "c", [(0, 1), (1, 0)])
    core = jnp.where(lax.axis_index("c") == 0, 0, 1).astype(jnp.int32).reshape(1)
    wide = wide.reshape(NX * NY, kn, part_d, cols)
    other = other.reshape(NX * NY, kn, part_d, cols)
    flat_gate = gate_w.reshape(din, tn * kn)

    gates, row_at, col_at = pl.pallas_call(
        gate_kernel(tn, kn, pair_slots),
        out_shape=(
            jax.ShapeDtypeStruct((rows, tn * kn), f32),
            jax.ShapeDtypeStruct((2 * tn, rows), f32),
            jax.ShapeDtypeStruct((rows, 2 * tn), f32),
        ),
        name="gates",
    )(inputs, flat_gate, sections.reshape(1, n_sec), tasks)

    vmem = pl.BlockSpec(memory_space=pltpu.VMEM)
    smem = pl.BlockSpec(memory_space=pltpu.SMEM)
    anym = pl.BlockSpec(memory_space=pl.ANY)
    w_scratch = [
        pltpu.VMEM((NX * NY, NC, kn, part_d, cols), bf16),
        pltpu.SemaphoreType.DMA((2,)),
    ]
    sent, pre = pl.pallas_call(
        forward_kernel(tn, kn, pair_slots, n_mp),
        out_shape=(
            jax.ShapeDtypeStruct((n_mp, slots, cols), bf16),
            jax.ShapeDtypeStruct((rows, kn * cols), f32),
        ),
        in_specs=[smem, anym, anym, vmem, vmem, vmem],
        out_specs=(vmem, vmem),
        scratch_shapes=w_scratch,
        name="experts",
    )(core, wide, other, inputs, gates, row_at)
    sent = sent.reshape(n_mp * n_sec, pair_slots, cols)
    arrived = lax.all_to_all(sent, ("mp",) + sec_axes, 0, 0, tiled=True)

    up = tower_up[0]
    out_w = tower_out[0].astype(f32)
    rows_in = arrived.reshape(n_mp, slots, cols).transpose(1, 0, 2).reshape(slots, width)
    act = jnp.dot(rows_in, up, preferred_element_type=f32)
    sig_act = jax.nn.sigmoid(act)
    logit_part = jnp.sum(act * sig_act * out_w[None, :], axis=1)
    act_grad = (out_w[None, :] * silu_slope(act, sig_act)).astype(bf16)
    back = lax.dot_general(
        act_grad, up, (((1,), (1,)), ((), ())), preferred_element_type=f32
    ).astype(bf16)
    back = back.reshape(slots, n_mp, cols).transpose(1, 0, 2)
    high, low = split_two(logit_part)
    extra = jnp.concatenate([high.reshape(-1, cols), low.reshape(-1, cols)], axis=0)
    n_extra = extra.shape[0]
    extra = jnp.concatenate([extra, jnp.zeros((16 - n_extra, cols), bf16)], axis=0)
    extra = jnp.broadcast_to(extra[None], (n_mp, 16, cols))
    summed = lax.all_to_all(jnp.concatenate([back, extra], axis=1), "mp", 0, 0, tiled=True)
    total = jnp.sum(summed.astype(f32), axis=0)
    logit = (total[slots : slots + n_extra // 2] + total[slots + n_extra // 2 : slots + n_extra])
    high, low = split_two(logit.reshape(n_sec, pair_slots))
    tail = jnp.concatenate([high, low], axis=1)
    tail = jnp.pad(tail, ((0, 0), (0, cols - 2 * pair_slots)))[:, None]
    body = total[:slots].astype(bf16).reshape(n_sec, pair_slots, cols)
    fill = jnp.zeros((n_sec, 8 - pair_slots - 1, cols), bf16)
    home = lax.all_to_all(
        jnp.concatenate([body, tail, fill], axis=1), sec_axes, 0, 0, tiled=True
    )
    partial = pl.pallas_call(
        backward_kernel(tn, kn, pair_slots, n_mp),
        out_shape=jax.ShapeDtypeStruct((n_mp, rows, din // n_mp), bf16),
        in_specs=[smem, anym, anym] + [vmem] * 7,
        out_specs=vmem,
        scratch_shapes=w_scratch,
        name="grads",
    )(
        core,
        wide,
        other,
        home.reshape(n_sec * 8, cols),
        gates,
        col_at,
        pre,
        labels,
        tasks,
        flat_gate,
    )
    pieces = lax.all_to_all(partial, "mp", 0, 0, tiled=True)
    return jnp.sum(pieces.astype(f32), axis=0).astype(bf16)


def solution(mesh):
    grid = Mesh(
        mesh.devices.reshape(NX, NY, NC, mesh.shape["mp"]), ("x", "y", "c", "mp")
    )
    sec = ("x", "y", "c")
    in_specs = (
        P(sec, None),
        P("mp", sec, None),
        P(),
        P(sec, None, "mp"),
        P(sec, "mp"),
        P(),
        P(sec, None),
        P(sec, None),
    )
    return jax.shard_map(
        per_device, mesh=grid, in_specs=in_specs, out_specs=P(sec, "mp"), check_vma=False
    )
```

```python
import jax
import jax.numpy as jnp
from jax import lax
from jax.experimental import pallas as pl
from jax.experimental.pallas import tpu as pltpu
from jax.sharding import Mesh, PartitionSpec as P

loss_scale = 64.0
NX, NY, NC = 4, 8, 2


def silu_slope(value, sig):
    return sig * (1.0 + value * (1.0 - sig))


def split_two(value):
    high = lax.reduce_precision(value, 8, 7)
    return high.astype(jnp.bfloat16), (value - high).astype(jnp.bfloat16)


def gate_kernel(tn, kn, pair_slots):
    f32, bf16 = jnp.float32, jnp.bfloat16

    def kernel(x_ref, gw_ref, sec_ref, task_ref, gate_ref, row_ref):
        logit = lax.dot_general(
            gw_ref[...], x_ref[...], (((1,), (1,)), ((), ())), preferred_element_type=f32
        )
        raised = jnp.exp(logit)
        for t in range(tn):
            part = raised[t * kn : (t + 1) * kn]
            gate_ref[t * kn : (t + 1) * kn, :] = part / jnp.sum(part, axis=0, keepdims=True)

        n_sec = sec_ref.shape[1]
        rows = task_ref.shape[1]
        sec_row = sec_ref[...]
        task = task_ref[...].astype(f32)
        one = lax.broadcasted_iota(jnp.int32, (rows, rows), 0)
        two = lax.broadcasted_iota(jnp.int32, (rows, rows), 1)
        above = (one < two).astype(f32).astype(bf16)
        rank = jnp.dot(task.astype(bf16), above, preferred_element_type=f32)
        ids = lax.broadcasted_iota(jnp.int32, (tn, n_sec), 0)
        member = jnp.sum((sec_row == ids).astype(f32), axis=1, keepdims=True)
        first = jnp.sum((sec_row < ids).astype(f32), axis=1, keepdims=True)
        turn = jnp.zeros_like(rank)
        for step in range(1, pair_slots):
            turn = turn + (rank >= step * member).astype(f32)
        target = first + rank - turn * member
        row_ref[0:tn, :] = jnp.where(task > 0.5, target, -1000.0)
        row_ref[tn : 2 * tn, :] = turn

    return kernel


def load_weights(core_ref, own_ref, other_ref, w_ref, sems):
    def run(own_at, finish):
        first = pltpu.make_async_copy(own_ref, w_ref.at[:, own_at], sems.at[0])
        second = pltpu.make_async_copy(other_ref, w_ref.at[:, 1 - own_at], sems.at[1])
        if finish:
            first.wait()
            second.wait()
        else:
            first.start()
            second.start()

    def both(finish):
        @pl.when(core_ref[0] == 0)
        def _():
            run(0, finish)

        @pl.when(core_ref[0] != 0)
        def _():
            run(1, finish)

    return lambda: both(False), lambda: both(True)


def pair_weights(w_ref, k, lo, hi):
    part_d, cols = w_ref.shape[3:]
    count = (hi - lo) * w_ref.shape[1] * part_d
    return jnp.concatenate(
        [w_ref[lo:hi, :, k + i].reshape(count, cols) for i in range(2)], axis=1
    )


def place_picks(row_ref, tn, total, stride, offsets):
    f32 = jnp.float32
    rows = row_ref.shape[1]
    slot_id = lax.broadcasted_iota(jnp.int32, (total, rows), 0).astype(f32)
    picks = []
    for t in range(tn):
        place = row_ref[t : t + 1, :] * stride + offsets(t)
        picks.append((slot_id == place).astype(f32).astype(jnp.bfloat16))
    return jnp.concatenate(picks, axis=1)


def forward_kernel(tn, kn, pair_slots, n_mp):
    f32, bf16 = jnp.float32, jnp.bfloat16

    def kernel(core_ref, own_ref, other_ref, x_ref, gate_ref, row_ref, sent_ref, pre_ref, w_ref, sems):
        start, wait = load_weights(core_ref, own_ref, other_ref, w_ref, sems)
        start()
        rows = x_ref.shape[0]
        slots, cols = sent_ref.shape[1:]
        pick = place_picks(
            row_ref, tn, slots, pair_slots, lambda t: row_ref[tn + t : tn + t + 1, :]
        )
        wait()
        x = x_ref[...]
        mix = [jnp.zeros((cols, rows), f32) for _ in range(tn)]
        for k in range(0, kn, 2):
            both = jnp.dot(
                x, pair_weights(w_ref, k, 0, w_ref.shape[0]), preferred_element_type=f32
            )
            for i in range(2):
                pre = both[:, i * cols : (i + 1) * cols].T
                pre_ref[k + i] = pre
                out = (pre * jax.nn.sigmoid(pre)).astype(bf16).astype(f32)
                for t in range(tn):
                    at = t * kn + k + i
                    mix[t] = mix[t] + gate_ref[at : at + 1, :] * out
        stack = jnp.concatenate([m.astype(bf16) for m in mix], axis=1)
        sent = lax.dot_general(
            pick, stack, (((1,), (1,)), ((), ())), preferred_element_type=f32
        ).astype(bf16)
        for m in range(n_mp):
            sent_ref[m] = sent

    return kernel


def backward_kernel(tn, kn, pair_slots, n_mp):
    f32, bf16 = jnp.float32, jnp.bfloat16

    def kernel(
        core_ref, own_ref, other_ref, home_ref, gate_ref, row_ref, pre_ref,
        label_ref, task_ref, gw_ref, out_ref, w_ref, sems,
    ):
        start, wait = load_weights(core_ref, own_ref, other_ref, w_ref, sems)
        start()
        total, cols = home_ref.shape
        rows = gate_ref.shape[1]
        home = home_ref[...]
        pick = place_picks(
            row_ref, tn, total, 8.0, lambda t: row_ref[tn + t : tn + t + 1, :]
        )
        pick_tail = place_picks(row_ref, tn, total, 8.0, lambda t: float(pair_slots))
        down = (((0,), (0,)), ((), ()))
        got = lax.dot_general(home, pick, down, preferred_element_type=f32)
        tail = lax.dot_general(home, pick_tail, down, preferred_element_type=f32)
        sub = lax.broadcasted_iota(jnp.int32, (8, rows), 0)
        grads = []
        for t in range(tn):
            turn = row_ref[tn + t : tn + t + 1, :].astype(jnp.int32)
            chosen = (sub == turn) | (sub == turn + pair_slots)
            part = tail[0:8, t * rows : (t + 1) * rows]
            logit = jnp.sum(jnp.where(chosen, part, 0.0), axis=0, keepdims=True)
            label = label_ref[t : t + 1, :].astype(f32)
            alive = task_ref[t : t + 1, :].astype(f32)
            slope = loss_scale * (jax.nn.sigmoid(logit) - label) * alive
            grads.append(
                (slope * got[:, t * rows : (t + 1) * rows]).astype(bf16).astype(f32)
            )
        sub_k = lax.broadcasted_iota(jnp.int32, (kn, rows), 0)
        gate_grads = [jnp.zeros((kn, rows), f32) for _ in range(tn)]
        pre_grads = []
        for k in range(kn):
            pre = pre_ref[k]
            sig = jax.nn.sigmoid(pre)
            out = (pre * sig).astype(bf16).astype(f32)
            grad = jnp.zeros((cols, rows), f32)
            for t in range(tn):
                at = t * kn + k
                grad = grad + gate_ref[at : at + 1, :] * grads[t]
                dot = jnp.sum(grads[t] * out, axis=0, keepdims=True)
                gate_grads[t] = jnp.where(sub_k == k, dot, gate_grads[t])
            pre_grads.append((grad * silu_slope(pre, sig)).T.astype(bf16))
        highs, lows = [], []
        for t in range(tn):
            gate = gate_ref[t * kn : (t + 1) * kn, :]
            spread = jnp.sum(gate * gate_grads[t], axis=0, keepdims=True)
            logit_grad = gate * (gate_grads[t] - spread)
            high = logit_grad.astype(bf16).astype(f32)
            highs.append(high)
            lows.append(logit_grad - high)
        blank = rows - 2 * tn * kn
        fill = [jnp.zeros((blank, rows), f32)]
        both = jnp.concatenate(highs + lows + fill, axis=0).T.astype(bf16)
        pre_grad = [jnp.concatenate(pre_grads[k : k + 2], axis=1) for k in range(0, kn, 2)]
        wait()
        per = w_ref.shape[0] // n_mp
        width = out_ref.shape[2]
        contract = (((1,), (1,)), ((), ()))
        for m in range(n_mp):
            gw = gw_ref[:, m * width : (m + 1) * width]
            gw = jnp.concatenate([gw, gw, jnp.zeros((blank, width), bf16)], axis=0)
            acc = jnp.dot(both, gw, preferred_element_type=f32)
            for k in range(0, kn, 2):
                w = pair_weights(w_ref, k, m * per, (m + 1) * per)
                acc = acc + lax.dot_general(
                    pre_grad[k // 2], w, contract, preferred_element_type=f32
                )
            out_ref[m] = acc.astype(bf16)

    return kernel


def per_device(inputs, expert_w, gate_w, tower_up, tower_out, sections, tasks, labels):
    f32, bf16 = jnp.float32, jnp.bfloat16
    rows, din = inputs.shape
    tn = tasks.shape[1]
    n_mp = lax.axis_size("mp")
    n_sec = NX * NY * NC
    kn = gate_w.shape[2]
    part_d, width = expert_w.shape[1:]
    cols = width // n_mp
    pair_slots = 2 * rows // n_sec
    slots = n_sec * pair_slots
    sec_axes = ("x", "y", "c")

    block = expert_w[0].reshape(part_d, n_mp, cols).transpose(1, 0, 2)
    block = jnp.broadcast_to(block[None], (NY, n_mp, part_d, cols))
    part = lax.all_to_all(
        block.reshape(NY * n_mp, part_d, cols), ("y", "mp"), 0, 0, tiled=True
    )
    wide = lax.all_to_all(
        jnp.broadcast_to(part[None], (NX,) + part.shape), "x", 0, 0, tiled=True
    )
    other = lax.ppermute(wide, "c", [(0, 1), (1, 0)])
    core = jnp.where(lax.axis_index("c") == 0, 0, 1).astype(jnp.int32).reshape(1)
    wide = wide.reshape(NX * NY, kn, part_d, cols)
    other = other.reshape(NX * NY, kn, part_d, cols)
    flat_gate = gate_w.transpose(1, 2, 0).reshape(tn * kn, din)
    task_rows = tasks.T

    gates, row_at = pl.pallas_call(
        gate_kernel(tn, kn, pair_slots),
        out_shape=(
            jax.ShapeDtypeStruct((tn * kn, rows), f32),
            jax.ShapeDtypeStruct((2 * tn, rows), f32),
        ),
        name="gates",
    )(inputs, flat_gate, sections.reshape(1, n_sec), task_rows)

    vmem = pl.BlockSpec(memory_space=pltpu.VMEM)
    smem = pl.BlockSpec(memory_space=pltpu.SMEM)
    anym = pl.BlockSpec(memory_space=pl.ANY)
    w_scratch = [
        pltpu.VMEM((NX * NY, NC, kn, part_d, cols), bf16),
        pltpu.SemaphoreType.DMA((2,)),
    ]
    sent, pre = pl.pallas_call(
        forward_kernel(tn, kn, pair_slots, n_mp),
        out_shape=(
            jax.ShapeDtypeStruct((n_mp, slots, cols), bf16),
            jax.ShapeDtypeStruct((kn, cols, rows), f32),
        ),
        in_specs=[smem, anym, anym, vmem, vmem, vmem],
        out_specs=(vmem, vmem),
        scratch_shapes=w_scratch,
        name="experts",
    )(core, wide, other, inputs, gates, row_at)
    sent = sent.reshape(n_mp * n_sec, pair_slots, cols)
    arrived = lax.all_to_all(sent, ("mp",) + sec_axes, 0, 0, tiled=True)

    up = tower_up[0]
    out_w = tower_out[0].astype(f32)
    rows_in = arrived.reshape(n_mp, slots, cols).transpose(1, 0, 2).reshape(slots, width)
    act = jnp.dot(rows_in, up, preferred_element_type=f32)
    sig_act = jax.nn.sigmoid(act)
    logit_part = jnp.sum(act * sig_act * out_w[None, :], axis=1)
    act_grad = (out_w[None, :] * silu_slope(act, sig_act)).astype(bf16)
    back = lax.dot_general(
        act_grad, up, (((1,), (1,)), ((), ())), preferred_element_type=f32
    ).astype(bf16)
    back = back.reshape(slots, n_mp, cols).transpose(1, 0, 2)
    high, low = split_two(logit_part)
    extra = jnp.concatenate([high.reshape(-1, cols), low.reshape(-1, cols)], axis=0)
    n_extra = extra.shape[0]
    extra = jnp.concatenate([extra, jnp.zeros((16 - n_extra, cols), bf16)], axis=0)
    extra = jnp.broadcast_to(extra[None], (n_mp, 16, cols))
    summed = lax.all_to_all(jnp.concatenate([back, extra], axis=1), "mp", 0, 0, tiled=True)
    total = jnp.sum(summed.astype(f32), axis=0)
    logit = (total[slots : slots + n_extra // 2] + total[slots + n_extra // 2 : slots + n_extra])
    high, low = split_two(logit.reshape(n_sec, pair_slots))
    tail = jnp.concatenate([high, low], axis=1)
    tail = jnp.pad(tail, ((0, 0), (0, cols - 2 * pair_slots)))[:, None]
    body = total[:slots].astype(bf16).reshape(n_sec, pair_slots, cols)
    fill = jnp.zeros((n_sec, 8 - pair_slots - 1, cols), bf16)
    home = lax.all_to_all(
        jnp.concatenate([body, tail, fill], axis=1), sec_axes, 0, 0, tiled=True
    )
    partial = pl.pallas_call(
        backward_kernel(tn, kn, pair_slots, n_mp),
        out_shape=jax.ShapeDtypeStruct((n_mp, rows, din // n_mp), bf16),
        in_specs=[smem, anym, anym] + [vmem] * 7,
        out_specs=vmem,
        scratch_shapes=w_scratch,
        name="grads",
    )(
        core,
        wide,
        other,
        home.reshape(n_sec * 8, cols),
        gates,
        row_at,
        pre,
        labels.T,
        task_rows,
        flat_gate,
    )
    pieces = lax.all_to_all(partial, "mp", 0, 0, tiled=True)
    return jnp.sum(pieces.astype(f32), axis=0).astype(bf16)


def solution(mesh):
    grid = Mesh(
        mesh.devices.reshape(NX, NY, NC, mesh.shape["mp"]), ("x", "y", "c", "mp")
    )
    sec = ("x", "y", "c")
    in_specs = (
        P(sec, None),
        P("mp", sec, None),
        P(),
        P(sec, None, "mp"),
        P(sec, "mp"),
        P(),
        P(sec, None),
        P(sec, None),
    )
    return jax.shard_map(
        per_device, mesh=grid, in_specs=in_specs, out_specs=P(sec, "mp"), check_vma=False
    )
```

```python
import jax
import jax.numpy as jnp
from jax import lax
from jax.experimental import pallas as pl
from jax.experimental.pallas import tpu as pltpu
from jax.sharding import Mesh, PartitionSpec as P

loss_scale = 64.0
NX, NY, NC = 4, 8, 2


def silu_slope(value, sig):
    return sig * (1.0 + value * (1.0 - sig))


def split_two(value):
    high = lax.reduce_precision(value, 8, 7)
    return high.astype(jnp.bfloat16), (value - high).astype(jnp.bfloat16)


def gate_kernel(tn, kn, pair_slots):
    f32, bf16 = jnp.float32, jnp.bfloat16

    def kernel(x_ref, gw_ref, sec_ref, task_ref, gate_ref, row_ref):
        logit = lax.dot_general(
            gw_ref[...], x_ref[...], (((1,), (1,)), ((), ())), preferred_element_type=f32
        )
        raised = jnp.exp(logit)
        for t in range(tn):
            part = raised[t * kn : (t + 1) * kn]
            gate_ref[t * kn : (t + 1) * kn, :] = part / jnp.sum(part, axis=0, keepdims=True)

        n_sec = sec_ref.shape[1]
        rows = task_ref.shape[1]
        sec_row = sec_ref[...]
        task = task_ref[...].astype(f32)
        one = lax.broadcasted_iota(jnp.int32, (rows, rows), 0)
        two = lax.broadcasted_iota(jnp.int32, (rows, rows), 1)
        above = (one < two).astype(f32).astype(bf16)
        rank = jnp.dot(task.astype(bf16), above, preferred_element_type=f32)
        ids = lax.broadcasted_iota(jnp.int32, (tn, n_sec), 0)
        member = jnp.sum((sec_row == ids).astype(f32), axis=1, keepdims=True)
        first = jnp.sum((sec_row < ids).astype(f32), axis=1, keepdims=True)
        turn = jnp.zeros_like(rank)
        for step in range(1, pair_slots):
            turn = turn + (rank >= step * member).astype(f32)
        target = first + rank - turn * member
        row_ref[0:tn, :] = jnp.where(task > 0.5, target, -1000.0)
        row_ref[tn : 2 * tn, :] = turn

    return kernel


def load_weights(core_ref, part_refs, w_ref, sems):
    n_y = part_refs[0].shape[0]

    def copies(pair):
        experts = pl.ds(2 * pair, 2)
        for i, part_ref in enumerate(part_refs):
            yield pltpu.make_async_copy(
                part_ref.at[:, experts],
                w_ref.at[pl.ds(core_ref[i % 4], n_y), core_ref[4 + i // 4], experts],
                sems.at[pair, i],
            )

    def start():
        for pair in range(w_ref.shape[2] // 2):
            for copy in copies(pair):
                copy.start()

    def wait(pair):
        for copy in copies(pair):
            copy.wait()

    return start, wait


def pair_weights(w_ref, k, lo, hi):
    part_d, cols = w_ref.shape[3:]
    count = (hi - lo) * w_ref.shape[1] * part_d
    return jnp.concatenate(
        [w_ref[lo:hi, :, k + i].reshape(count, cols) for i in range(2)], axis=1
    )


def place_picks(row_ref, tn, total, stride, offsets):
    f32 = jnp.float32
    rows = row_ref.shape[1]
    slot_id = lax.broadcasted_iota(jnp.int32, (total, rows), 0).astype(f32)
    picks = []
    for t in range(tn):
        place = row_ref[t : t + 1, :] * stride + offsets(t)
        picks.append((slot_id == place).astype(f32).astype(jnp.bfloat16))
    return jnp.concatenate(picks, axis=1)


def forward_kernel(tn, kn, pair_slots, n_mp):
    f32, bf16 = jnp.float32, jnp.bfloat16

    def kernel(core_ref, *refs):
        x_ref, gate_ref, row_ref, sent_ref, pre_ref, w_ref, sems = refs[8:]
        start, wait = load_weights(core_ref, refs[:8], w_ref, sems)
        start()
        rows = x_ref.shape[0]
        slots, cols = sent_ref.shape[1:]
        pick = place_picks(
            row_ref, tn, slots, pair_slots, lambda t: row_ref[tn + t : tn + t + 1, :]
        )
        x = x_ref[...]
        mix = [jnp.zeros((cols, rows), f32) for _ in range(tn)]
        for k in range(0, kn, 2):
            wait(k // 2)
            both = jnp.dot(
                x, pair_weights(w_ref, k, 0, w_ref.shape[0]), preferred_element_type=f32
            )
            for i in range(2):
                pre = both[:, i * cols : (i + 1) * cols].T
                pre_ref[k + i] = pre
                out = (pre * jax.nn.sigmoid(pre)).astype(bf16).astype(f32)
                for t in range(tn):
                    at = t * kn + k + i
                    mix[t] = mix[t] + gate_ref[at : at + 1, :] * out
        stack = jnp.concatenate([m.astype(bf16) for m in mix], axis=1)
        sent = lax.dot_general(
            pick, stack, (((1,), (1,)), ((), ())), preferred_element_type=f32
        ).astype(bf16)
        for m in range(n_mp):
            sent_ref[m] = sent

    return kernel


def backward_kernel(tn, kn, pair_slots, n_mp):
    f32, bf16 = jnp.float32, jnp.bfloat16

    def kernel(core_ref, *refs):
        home_ref, gate_ref, row_ref, pre_ref, label_ref, task_ref, gw_ref = refs[8:15]
        out_ref, w_ref, sems = refs[15:]
        start, wait = load_weights(core_ref, refs[:8], w_ref, sems)
        start()
        total, cols = home_ref.shape
        rows = gate_ref.shape[1]
        home = home_ref[...]
        pick = place_picks(
            row_ref, tn, total, 8.0, lambda t: row_ref[tn + t : tn + t + 1, :]
        )
        pick_tail = place_picks(row_ref, tn, total, 8.0, lambda t: float(pair_slots))
        down = (((0,), (0,)), ((), ()))
        got = lax.dot_general(home, pick, down, preferred_element_type=f32)
        tail = lax.dot_general(home, pick_tail, down, preferred_element_type=f32)
        sub = lax.broadcasted_iota(jnp.int32, (8, rows), 0)
        grads = []
        for t in range(tn):
            turn = row_ref[tn + t : tn + t + 1, :].astype(jnp.int32)
            chosen = (sub == turn) | (sub == turn + pair_slots)
            part = tail[0:8, t * rows : (t + 1) * rows]
            logit = jnp.sum(jnp.where(chosen, part, 0.0), axis=0, keepdims=True)
            label = label_ref[t : t + 1, :].astype(f32)
            alive = task_ref[t : t + 1, :].astype(f32)
            slope = loss_scale * (jax.nn.sigmoid(logit) - label) * alive
            grads.append(
                (slope * got[:, t * rows : (t + 1) * rows]).astype(bf16).astype(f32)
            )
        sub_k = lax.broadcasted_iota(jnp.int32, (kn, rows), 0)
        gate_grads = [jnp.zeros((kn, rows), f32) for _ in range(tn)]
        pre_grads = []
        for k in range(kn):
            pre = pre_ref[k]
            sig = jax.nn.sigmoid(pre)
            out = (pre * sig).astype(bf16).astype(f32)
            grad = jnp.zeros((cols, rows), f32)
            for t in range(tn):
                at = t * kn + k
                grad = grad + gate_ref[at : at + 1, :] * grads[t]
                dot = jnp.sum(grads[t] * out, axis=0, keepdims=True)
                gate_grads[t] = jnp.where(sub_k == k, dot, gate_grads[t])
            pre_grads.append((grad * silu_slope(pre, sig)).T.astype(bf16))
        highs, lows = [], []
        for t in range(tn):
            gate = gate_ref[t * kn : (t + 1) * kn, :]
            spread = jnp.sum(gate * gate_grads[t], axis=0, keepdims=True)
            logit_grad = gate * (gate_grads[t] - spread)
            high = logit_grad.astype(bf16).astype(f32)
            highs.append(high)
            lows.append(logit_grad - high)
        blank = rows - 2 * tn * kn
        fill = [jnp.zeros((blank, rows), f32)]
        both = jnp.concatenate(highs + lows + fill, axis=0).T.astype(bf16)
        pre_grad = [jnp.concatenate(pre_grads[k : k + 2], axis=1) for k in range(0, kn, 2)]
        for pair in range(kn // 2):
            wait(pair)
        per = w_ref.shape[0] // n_mp
        width = out_ref.shape[2]
        contract = (((1,), (1,)), ((), ()))
        for m in range(n_mp):
            gw = gw_ref[:, m * width : (m + 1) * width]
            gw = jnp.concatenate([gw, gw, jnp.zeros((blank, width), bf16)], axis=0)
            acc = jnp.dot(both, gw, preferred_element_type=f32)
            for k in range(0, kn, 2):
                w = pair_weights(w_ref, k, m * per, (m + 1) * per)
                acc = acc + lax.dot_general(
                    pre_grad[k // 2], w, contract, preferred_element_type=f32
                )
            out_ref[m] = acc.astype(bf16)

    return kernel


def per_device(inputs, expert_w, gate_w, tower_up, tower_out, sections, tasks, labels):
    f32, bf16 = jnp.float32, jnp.bfloat16
    rows, din = inputs.shape
    tn = tasks.shape[1]
    n_mp = lax.axis_size("mp")
    n_sec = NX * NY * NC
    kn = gate_w.shape[2]
    part_d, width = expert_w.shape[1:]
    cols = width // n_mp
    pair_slots = 2 * rows // n_sec
    slots = n_sec * pair_slots
    sec_axes = ("x", "y", "c")

    block = expert_w[0].reshape(part_d, n_mp, cols).transpose(1, 0, 2)
    block = jnp.broadcast_to(block[None], (NY, n_mp, part_d, cols))
    part = lax.all_to_all(
        block.reshape(NY * n_mp, part_d, cols), ("y", "mp"), 0, 0, tiled=True
    )
    blocks = part.reshape(NY, kn, part_d, cols)
    half = NY // 2
    ahead = [(i, (i + 1) % NX) for i in range(NX)]
    behind = [((i + 1) % NX, i) for i in range(NX)]
    swap = [(0, 1), (1, 0)]
    prev = lax.ppermute(blocks, "x", ahead)
    succ = lax.ppermute(blocks, "x", behind)
    far_low = lax.ppermute(prev[:half], "x", ahead)
    far_high = lax.ppermute(succ[half:], "x", behind)
    far = jnp.concatenate([far_low, far_high], axis=0)
    own = [blocks, prev, succ, far]
    other = [lax.ppermute(piece, "c", swap) for piece in own]
    weights = own + other
    at_x, at_c = lax.axis_index("x"), lax.axis_index("c")
    spots = jnp.stack([at_x, at_x + NX - 1, at_x + 1, at_x + 2]) % NX
    core = jnp.concatenate([spots * NY, at_c[None], 1 - at_c[None]]).astype(jnp.int32)
    flat_gate = gate_w.transpose(1, 2, 0).reshape(tn * kn, din)
    task_rows = tasks.T

    gates, row_at = pl.pallas_call(
        gate_kernel(tn, kn, pair_slots),
        out_shape=(
            jax.ShapeDtypeStruct((tn * kn, rows), f32),
            jax.ShapeDtypeStruct((2 * tn, rows), f32),
        ),
        name="gates",
    )(inputs, flat_gate, sections.reshape(1, n_sec), task_rows)

    vmem = pl.BlockSpec(memory_space=pltpu.VMEM)
    smem = pl.BlockSpec(memory_space=pltpu.SMEM)
    anym = pl.BlockSpec(memory_space=pl.ANY)
    w_scratch = [
        pltpu.VMEM((NX * NY, NC, kn, part_d, cols), bf16),
        pltpu.SemaphoreType.DMA((kn // 2, 8)),
    ]
    sent, pre = pl.pallas_call(
        forward_kernel(tn, kn, pair_slots, n_mp),
        out_shape=(
            jax.ShapeDtypeStruct((n_mp, slots, cols), bf16),
            jax.ShapeDtypeStruct((kn, cols, rows), f32),
        ),
        in_specs=[smem] + [anym] * 8 + [vmem] * 3,
        out_specs=(vmem, vmem),
        scratch_shapes=w_scratch,
        name="experts",
    )(core, *weights, inputs, gates, row_at)
    sent = sent.reshape(n_mp * n_sec, pair_slots, cols)
    arrived = lax.all_to_all(sent, ("mp",) + sec_axes, 0, 0, tiled=True)

    up = tower_up[0]
    out_w = tower_out[0].astype(f32)
    rows_in = arrived.reshape(n_mp, slots, cols).transpose(1, 0, 2).reshape(slots, width)
    act = jnp.dot(rows_in, up, preferred_element_type=f32)
    sig_act = jax.nn.sigmoid(act)
    logit_part = jnp.sum(act * sig_act * out_w[None, :], axis=1)
    act_grad = (out_w[None, :] * silu_slope(act, sig_act)).astype(bf16)
    back = lax.dot_general(
        act_grad, up, (((1,), (1,)), ((), ())), preferred_element_type=f32
    ).astype(bf16)
    back = back.reshape(slots, n_mp, cols).transpose(1, 0, 2)
    high, low = split_two(logit_part)
    extra = jnp.concatenate([high.reshape(-1, cols), low.reshape(-1, cols)], axis=0)
    n_extra = extra.shape[0]
    extra = jnp.concatenate([extra, jnp.zeros((16 - n_extra, cols), bf16)], axis=0)
    extra = jnp.broadcast_to(extra[None], (n_mp, 16, cols))
    summed = lax.all_to_all(jnp.concatenate([back, extra], axis=1), "mp", 0, 0, tiled=True)
    total = jnp.sum(summed.astype(f32), axis=0)
    logit = (total[slots : slots + n_extra // 2] + total[slots + n_extra // 2 : slots + n_extra])
    high, low = split_two(logit.reshape(n_sec, pair_slots))
    tail = jnp.concatenate([high, low], axis=1)
    tail = jnp.pad(tail, ((0, 0), (0, cols - 2 * pair_slots)))[:, None]
    body = total[:slots].astype(bf16).reshape(n_sec, pair_slots, cols)
    fill = jnp.zeros((n_sec, 8 - pair_slots - 1, cols), bf16)
    home = lax.all_to_all(
        jnp.concatenate([body, tail, fill], axis=1), sec_axes, 0, 0, tiled=True
    )
    partial = pl.pallas_call(
        backward_kernel(tn, kn, pair_slots, n_mp),
        out_shape=jax.ShapeDtypeStruct((n_mp, rows, din // n_mp), bf16),
        in_specs=[smem] + [anym] * 8 + [vmem] * 7,
        out_specs=vmem,
        scratch_shapes=w_scratch,
        name="grads",
    )(
        core,
        *weights,
        home.reshape(n_sec * 8, cols),
        gates,
        row_at,
        pre,
        labels.T,
        task_rows,
        flat_gate,
    )
    pieces = lax.all_to_all(partial, "mp", 0, 0, tiled=True)
    return jnp.sum(pieces.astype(f32), axis=0).astype(bf16)


def solution(mesh):
    grid = Mesh(
        mesh.devices.reshape(NX, NY, NC, mesh.shape["mp"]), ("x", "y", "c", "mp")
    )
    sec = ("x", "y", "c")
    in_specs = (
        P(sec, None),
        P("mp", sec, None),
        P(),
        P(sec, None, "mp"),
        P(sec, "mp"),
        P(),
        P(sec, None),
        P(sec, None),
    )
    return jax.shard_map(
        per_device, mesh=grid, in_specs=in_specs, out_specs=P(sec, "mp"), check_vma=False
    )
```
